256 devices in a mesh: band: 16 (over y, x), wall: 16 (over z, core).
Axes of the slice: x: 4, y: 4, z: 8, core: 2. Of those that a mesh axis runs over, the one named last changes fastest.
Arguments:
- state_in: float32 [5, 128, 32, 128], P(None, 'wall', 'band'), may hold values from -8 to 8
- source: float32 [5, 128, 32, 128], P(None, 'wall', 'band'), may hold values from -0.05 to 0.05
- face_flux: float32 [5, 5, 128, 32, 128], P(None, None, 'wall', 'band'), may hold values from -1.6 to 16, as said below
- time_term: float32 [5, 128, 32, 128], P(None, 'wall', 'band'), may hold values from 0.0003 to 0.003
- inplane_coef: float32 [2, 128, 32, 128], P(None, 'wall', 'band'), may hold values from 0.0001 to 0.0006
Outputs:
- state_out: float32 [5, 128, 32, 128], P(None, 'wall', 'band')
The draws below stay inside these ranges and needn't reach their ends.
Inputs may be any that keep to these rules, and one draw needn't show every extreme that they name: `face_flux`: every 5x5 block is s (G + E) with s > 0 a scale of its cell, G diagonal with entries in 1 to 2, and E zero on the diagonal with entries of magnitude at most 0.2.
All inputs are finite; a program needn't handle non-finite values.
Results may differ from the reference program's by a relative error of at most 0.0003.
Values sent between devices are 32-bit elements; how exact they have to be, the bound alone decides.
A program may use at most 64 MiB of HBM per device.

```python
import math
import jax
import jax.numpy as jnp
from jax import lax

J = 128
SWEEPS = 2
NK = 128
NI = 32


def draw_source(key, part):
    values = 0.01 * jax.random.truncated_normal(key, -5.0, 5.0, (5, NK, NI, J), jnp.float32)
    return values.astype(jnp.float32)


def draw_face_flux(key, part):
    key_scale, key_off, key_diag = jax.random.split(key, 3)
    log_top = jnp.log(4.0)
    scale = jnp.exp(jax.random.uniform(key_scale, (1, 1, NK, NI, J), jnp.float32, 0.0, 1.0) * log_top)
    entries = jax.random.uniform(key_off, (5, 5, NK, NI, J), jnp.float32, -0.2, 0.2)
    diagonal = jax.random.uniform(key_diag, (5, NK, NI, J), jnp.float32, 1.0, 2.0)
    identity = jnp.eye(5, dtype=jnp.float32)[:, :, None, None, None]
    blocks = scale * (entries * (1.0 - identity) + identity * diagonal[:, None])
    return blocks.astype(jnp.float32)


def block_levels(own_key, dims, cuts, smallest, high):
    factor_of, own = 1.0, jax.random.fold_in(own_key, 6)
    for position, parts in cuts:
        steps = jnp.exp(jax.random.uniform(jax.random.fold_in(own, position), (parts,), jnp.float32, smallest / len(cuts), high / len(cuts)))
        factor_of = factor_of * jnp.repeat(steps, dims[position] // parts).reshape([-1 if axis == position else 1 for axis in range(len(dims))])
    return factor_of


def bell_draw(own_key, extent, scale, most, cuts=(), held_as=jnp.bfloat16):
    array = jax.random.normal(own_key, extent, jnp.float32) * scale
    if len(cuts) > 0:
        array = block_levels(own_key, extent, cuts, -0.22, 0.18) * array
    return jnp.clip(array, min=-most, max=most).astype(held_as)


def setup_inputs(seed: int = 0) -> dict:
    splits = jax.random.split(jax.random.key(seed), 6)
    state_in = bell_draw(splits[0], (5, NK, NI, J), 2.0, 8.0, ((1, 16), (2, 16)), jnp.float32)
    source = draw_source(jax.random.fold_in(splits[5], 71), 0)
    face_flux = draw_face_flux(jax.random.fold_in(splits[5], 71), 0)
    time_term = jnp.clip(jnp.exp(math.log(0.003) - 2.3025851 * jax.random.uniform(splits[3], (5, NK, NI, J), jnp.float32) ** block_levels(splits[3], (5, NK, NI, J), ((1, 16), (2, 16)), -0.2, 0.2)), 0.0003, 0.003)
    inplane_coef = jnp.clip(jnp.exp(math.log(0.0006) - 1.7917595 * jax.random.uniform(splits[4], (2, NK, NI, J), jnp.float32) ** block_levels(splits[4], (2, NK, NI, J), ((1, 16), (2, 16)), -0.2, 0.2)), 0.0001, 0.0006)
    return dict(state_in=state_in, source=source, face_flux=face_flux, time_term=time_term, inplane_coef=inplane_coef)


def apply_blocks(blocks, field):
    return jnp.sum(blocks * field[None, :], axis=1)

def line_blocks(face_flux, time_term, inplane_coef):
    zero_layer = jnp.zeros_like(face_flux[:, :, :1])
    upper_face = jnp.concatenate([face_flux[:, :, 1:], zero_layer], axis=2)
    lower = -jnp.concatenate([zero_layer, face_flux[:, :, 1:]], axis=2)
    center = time_term + 2.5 * (inplane_coef[0] + inplane_coef[1])
    identity = jnp.eye(5, dtype=jnp.float32)[:, :, None, None, None]
    middle = face_flux + upper_face + identity * center[:, None]
    return (lower, middle, -upper_face)

def inplane(field, inplane_coef):
    wide_i = jnp.pad(field, ((0, 0), (0, 0), (2, 2), (0, 0)))
    wide_j = jnp.pad(field, ((0, 0), (0, 0), (0, 0), (2, 2)))
    along_i = 1.0 / 12.0 * (wide_i[:, :, 4:] + wide_i[:, :, :-4]) - 4.0 / 3.0 * (wide_i[:, :, 3:-1] + wide_i[:, :, 1:-3])
    along_j = 1.0 / 12.0 * (wide_j[:, :, :, 4:] + wide_j[:, :, :, :-4]) - 4.0 / 3.0 * (wide_j[:, :, :, 3:-1] + wide_j[:, :, :, 1:-3])
    return inplane_coef[0] * along_i + inplane_coef[1] * along_j

def operate(field, lower, middle, upper, inplane_coef):
    zero_layer = jnp.zeros_like(field[:, :1])
    below = jnp.concatenate([zero_layer, field[:, :-1]], axis=1)
    above = jnp.concatenate([field[:, 1:], zero_layer], axis=1)
    return apply_blocks(lower, below) + apply_blocks(middle, field) + apply_blocks(upper, above) + inplane(field, inplane_coef)

def line_solve(lower, middle, upper, target):
    order_blocks = (2, 3, 4, 0, 1)
    lower_rows = jnp.transpose(lower, order_blocks)
    middle_rows = jnp.transpose(middle, order_blocks)
    upper_rows = jnp.transpose(upper, order_blocks)
    target_rows = jnp.transpose(target, (1, 2, 3, 0))
    highest = lax.Precision.HIGHEST

    def forward(carry, slab):
        factor_prev, value_prev = carry
        low_here, mid_here, up_here, tgt_here = slab
        pivot = mid_here - jnp.matmul(low_here, factor_prev, precision=highest)
        factor = jnp.linalg.solve(pivot, up_here)
        shifted = tgt_here - jnp.matmul(low_here, value_prev[..., None], precision=highest)[..., 0]
        value = jnp.linalg.solve(pivot, shifted[..., None])[..., 0]
        return ((factor, value), (factor, value))
    start = (jnp.zeros(lower_rows.shape[1:], jnp.float32), jnp.zeros(target_rows.shape[1:], jnp.float32))
    _, (factors, values) = lax.scan(forward, start, (lower_rows, middle_rows, upper_rows, target_rows))

    def backward(carry, slab):
        factor, value = slab
        result = value - jnp.matmul(factor, carry[..., None], precision=highest)[..., 0]
        return (result, result)
    _, solved = lax.scan(backward, jnp.zeros(target_rows.shape[1:], jnp.float32), (factors, values), reverse=True)
    return jnp.transpose(solved, (3, 0, 1, 2))

def reference(state_in, source, face_flux, time_term, inplane_coef):
    lower, middle, upper = line_blocks(face_flux, time_term, inplane_coef)
    state = state_in
    for sweep in range(SWEEPS):
        residual = source - operate(state, lower, middle, upper, inplane_coef)
        state = state + line_solve(lower, middle, upper, residual)
    return state
```

```python
import jax
import jax.numpy as jnp
from jax import lax
from jax.experimental import pallas as pl
from jax.experimental.pallas import tpu as pltpu
from jax.sharding import PartitionSpec as P

SWEEPS = 2
N = 5
CELLS = 8
INNER = CELLS - 1
SEGS = 16
MATRIX_GROUPS = 13
VECTOR_GROUPS = 2
MATRIX_ROWS = 16
VECTOR_ROWS = 8
MESH = pl.DeviceIdType.MESH


def matmul(left, right):
    total = left[:, 0:1] * right[0:1]
    for k in range(1, N):
        total = total + left[:, k : k + 1] * right[k : k + 1]
    return total


def matvec(matrix, vector):
    total = matrix[:, 0] * vector[0:1]
    for k in range(1, N):
        total = total + matrix[:, k] * vector[k : k + 1]
    return total


def with_entry(row, at, value):
    parts = []
    if at > 0:
        parts.append(row[:at])
    parts.append(value)
    if at < N - 1:
        parts.append(row[at + 1 :])
    return jnp.concatenate(parts, axis=0)


def invert(matrix):
    rows = [matrix[i] for i in range(N)]
    zero = jnp.zeros_like(rows[0][0:1])
    for p in range(N):
        scale = 1.0 / rows[p][p : p + 1]
        pivot_row = with_entry(rows[p] * scale, p, scale)
        updated = []
        for i in range(N):
            if i == p:
                updated.append(pivot_row)
            else:
                column = rows[i][p : p + 1]
                updated.append(with_entry(rows[i], p, zero) - column * pivot_row)
        rows = updated
    return jnp.stack(rows, axis=0)


def add_diagonal(matrix, diagonal):
    rows = [
        with_entry(matrix[i], i, matrix[i][i : i + 1] + diagonal[i : i + 1]) for i in range(N)
    ]
    return jnp.stack(rows, axis=0)


def one_minus(matrix):
    rows = [with_entry(-matrix[i], i, 1.0 - matrix[i][i : i + 1]) for i in range(N)]
    return jnp.stack(rows, axis=0)


def swap_rows(values):
    return jnp.concatenate([values[..., 1:2, :], values[..., 0:1, :]], axis=-2)


def lane_roll(values, shift):
    return pltpu.roll(values, shift % 128, values.ndim - 1)


def lane_of(values):
    return lax.broadcasted_iota(jnp.int32, values.shape, values.ndim - 1)


def row_of(values):
    return lax.broadcasted_iota(jnp.int32, values.shape, values.ndim - 2)


def segment_before(values, distance):
    if distance == 8:
        return swap_rows(values)
    rolled = lane_roll(values, 16 * distance)
    return jnp.where(lane_of(values) < 16 * distance, swap_rows(rolled), rolled)


def segment_after(values, distance):
    if distance == 8:
        return swap_rows(values)
    rolled = lane_roll(values, -16 * distance)
    return jnp.where(lane_of(values) >= 128 - 16 * distance, swap_rows(rolled), rolled)


def first_segment(values):
    return (row_of(values) == 0) & (lane_of(values) < 16)


def last_segment(values):
    return (row_of(values) == 1) & (lane_of(values) >= 112)


def transpose_groups(tile):
    sublane = row_of(tile)
    group = lane_of(tile) // 16
    for bit in (1, 2, 4):
        in_row = (sublane // bit) % 2 == 1
        in_lane = (group // bit) % 2 == 1
        from_next = lane_roll(pltpu.roll(tile, 8 - bit, 0), 16 * bit)
        if bit == 4:
            other = from_next
        else:
            from_prev = lane_roll(pltpu.roll(tile, bit, 0), -16 * bit)
            other = jnp.where(in_lane, from_next, from_prev)
        tile = jnp.where(in_row == in_lane, tile, other)
    return tile


def pack(fields, messages, groups, rows):
    for g in range(groups):
        for r in range(2):
            tile = fields[pl.ds(16 * g + r, 8, stride=2), :]
            messages[pl.ds(8 * r * rows + g, 8, stride=rows), :] = transpose_groups(tile)


def unpack(messages, fields, groups, rows):
    for g in range(groups):
        for r in range(2):
            tile = messages[pl.ds(8 * r * rows + g, 8, stride=rows), :]
            fields[pl.ds(16 * g + r, 8, stride=2), :] = transpose_groups(tile)


def put_vector(fields, first, vector):
    for i in range(N):
        at = 2 * (first + i)
        fields[at : at + 2, :] = vector[i]


def get_vector(fields, first):
    return jnp.stack([fields[2 * (first + i) : 2 * (first + i) + 2, :] for i in range(N)], axis=0)


def put_matrix(fields, first, matrix):
    for i in range(N):
        put_vector(fields, first + N * i, matrix[i])


def get_matrix(fields, first):
    return jnp.stack([get_vector(fields, first + N * i) for i in range(N)], axis=0)


def kernel(
    state_in,
    source_in,
    face_in,
    time_in,
    coef_in,
    out,
    state,
    source,
    face,
    time,
    coef,
    held_inverse,
    held_lower,
    held_upper,
    spike_low,
    spike_high,
    partial,
    chain_inverse,
    round_inverse,
    round_lower,
    round_upper,
    matrix_fields,
    vector_fields,
    matrix_out,
    matrix_in,
    vector_out,
    vector_in,
    halo_in,
    load_sem,
    matrix_send,
    matrix_recv,
    vector_send,
    vector_recv,
    halo_send,
    halo_recv,
):
    wall = lax.axis_index("wall")
    band = lax.axis_index("band")
    bands = lax.axis_size("band")
    band_prev = lax.rem(band + bands - 1, bands)
    band_next = lax.rem(band + 1, bands)

    barrier = pltpu.get_barrier_semaphore()
    for neighbour in (band_prev, band_next):
        pl.semaphore_signal(barrier, inc=1, device_id={"band": neighbour}, device_id_type=MESH)
    for offset in range(1, SEGS):
        pl.semaphore_signal(
            barrier,
            inc=1,
            device_id={"wall": lax.rem(wall + offset, SEGS)},
            device_id_type=MESH,
        )

    loads = [
        pltpu.make_async_copy(face_in, face, load_sem.at[0]),
        pltpu.make_async_copy(time_in, time, load_sem.at[1]),
        pltpu.make_async_copy(coef_in, coef, load_sem.at[2]),
        pltpu.make_async_copy(state_in, state, load_sem.at[3]),
        pltpu.make_async_copy(source_in, source, load_sem.at[4]),
    ]
    for load in loads:
        load.start()

    def exchange(send_from, land_in, send_sems, recv_sems, rows):
        copies = []
        for offset in range(1, SEGS):
            there = lax.rem(wall + offset, SEGS)
            copy = pltpu.make_async_remote_copy(
                src_ref=send_from.at[pl.ds(pl.multiple_of(there * rows, rows), rows)],
                dst_ref=land_in.at[pl.ds(pl.multiple_of(wall * rows, rows), rows)],
                send_sem=send_sems.at[offset],
                recv_sem=recv_sems.at[offset],
                device_id={"wall": there},
                device_id_type=MESH,
            )
            copy.start()
            copies.append(copy)
        own = pl.ds(pl.multiple_of(wall * rows, rows), rows)
        land_in[own, :] = send_from[own, :]
        return copies

    def exchange_halo(turn):
        copies = []
        for side, there in ((0, band_next), (1, band_prev)):
            copy = pltpu.make_async_remote_copy(
                src_ref=state,
                dst_ref=halo_in.at[turn, side],
                send_sem=halo_send.at[turn, side],
                recv_sem=halo_recv.at[turn, side],
                device_id={"band": there},
                device_id_type=MESH,
            )
            copy.start()
            copies.append(copy)
        return copies

    for load in loads[:3]:
        load.wait()

    upper = None
    spike = None
    for m in range(INNER):
        own_face = face[:, :, m]
        next_face = face[:, :, m + 1]
        center = time[:, m] + 2.5 * (coef[0:1, m] + coef[1:2, m])
        if m == 0:
            pivot = own_face + next_face
        else:
            pivot = next_face + matmul(own_face, one_minus(upper))
        inverse = invert(add_diagonal(pivot, center))
        lower = matmul(inverse, own_face)
        upper = matmul(inverse, next_face)
        spike = lower if m == 0 else matmul(lower, spike)
        held_inverse[m] = inverse
        held_lower[m] = lower
        held_upper[m] = upper
        spike_low[m] = spike
    spike_high[INNER - 1] = upper
    high = upper
    for m in range(INNER - 2, -1, -1):
        upper = held_upper[m]
        spike = spike_low[m] + matmul(upper, spike)
        high = matmul(upper, high)
        spike_low[m] = spike
        spike_high[m] = high

    first_face = face[:, :, 0]
    last_face = face[:, :, INNER]
    center = time[:, INNER] + 2.5 * (coef[0:1, INNER] + coef[1:2, INNER])
    put_matrix(matrix_fields, 0, matmul(first_face, one_minus(spike)))
    put_matrix(matrix_fields, 25, -matmul(first_face, high))
    put_matrix(matrix_fields, 50, -matmul(last_face, spike_low[INNER - 1]))
    put_matrix(
        matrix_fields,
        75,
        add_diagonal(matmul(last_face, one_minus(spike_high[INNER - 1])), center),
    )

    for load in loads[3:]:
        load.wait()
    pl.semaphore_wait(barrier, SEGS + 1)
    pending = exchange_halo(0)
    pack(matrix_fields, matrix_out, MATRIX_GROUPS, MATRIX_ROWS)
    matrix_copies = exchange(matrix_out, matrix_in, matrix_send, matrix_recv, MATRIX_ROWS)

    has_prev = jnp.where(band > 0, 1.0, 0.0).astype(jnp.float32)
    has_next = jnp.where(band < bands - 1, 1.0, 0.0).astype(jnp.float32)

    def eliminate(turn):
        value = None
        for m in range(CELLS):
            here = state[:, m]
            before = halo_in[turn, 0, :, m] * has_prev
            after = halo_in[turn, 1, :, m] * has_next
            top = row_of(here) == 0
            along_i = (1.0 / 12.0) * (before + after) - (4.0 / 3.0) * swap_rows(
                here + jnp.where(top, after, before)
            )
            lane = lane_of(here)
            far = jnp.where(lane < 126, lane_roll(here, -2), 0.0) + jnp.where(
                lane >= 2, lane_roll(here, 2), 0.0
            )
            near = jnp.where(lane < 127, lane_roll(here, -1), 0.0) + jnp.where(
                lane >= 1, lane_roll(here, 1), 0.0
            )
            along_j = (1.0 / 12.0) * far - (4.0 / 3.0) * near
            target = source[:, m] - (coef[0:1, m] * along_i + coef[1:2, m] * along_j)
            if m == INNER:
                put_vector(vector_fields, N, target + matvec(face[:, :, INNER], value))
            else:
                fresh = matvec(held_inverse[m], target)
                value = fresh if m == 0 else fresh + matvec(held_lower[m], value)
                partial[m] = value
        for m in range(INNER - 2, -1, -1):
            value = partial[m] + matvec(held_upper[m], value)
            partial[m] = value
        put_vector(vector_fields, 0, matvec(face[:, :, 0], value))

    def factor_chain():
        from_above = []
        for first in (0, 25):
            block = segment_after(get_matrix(matrix_fields, first), 1)
            from_above.append(jnp.where(last_segment(block), 0.0, block))
        lower = get_matrix(matrix_fields, 50)
        lower = jnp.where(first_segment(lower), 0.0, lower)
        inverse = invert(get_matrix(matrix_fields, 75) + from_above[0])
        chain_inverse[...] = inverse
        lower = matmul(inverse, lower)
        upper = matmul(inverse, from_above[1])
        for step, distance in enumerate((1, 2, 4, 8)):
            upper_before = segment_before(upper, distance)
            lower_after = segment_after(lower, distance)
            inverse = invert(
                one_minus(matmul(lower, upper_before) + matmul(upper, lower_after))
            )
            low = matmul(inverse, lower)
            high = matmul(inverse, upper)
            round_inverse[step] = inverse
            round_lower[step] = low
            round_upper[step] = high
            if distance < 8:
                lower = -matmul(low, segment_before(lower, distance))
                upper = -matmul(high, segment_after(upper, distance))

    def solve_chain():
        from_above = segment_after(get_vector(vector_fields, 0), 1)
        from_above = jnp.where(last_segment(from_above), 0.0, from_above)
        value = matvec(chain_inverse[...], get_vector(vector_fields, N) + from_above)
        for step, distance in enumerate((1, 2, 4, 8)):
            value = (
                matvec(round_inverse[step], value)
                - matvec(round_lower[step], segment_before(value, distance))
                - matvec(round_upper[step], segment_after(value, distance))
            )
        before = segment_before(value, 1)
        put_vector(vector_fields, 0, jnp.where(first_segment(before), 0.0, before))
        put_vector(vector_fields, N, value)

    for turn in range(SWEEPS):
        for copy in pending:
            copy.wait()
        eliminate(turn)
        trips = []
        trip = 2 * turn
        pack(vector_fields, vector_out.at[trip], VECTOR_GROUPS, VECTOR_ROWS)
        trips.append(
            exchange(
                vector_out.at[trip],
                vector_in.at[trip],
                vector_send.at[trip],
                vector_recv.at[trip],
                VECTOR_ROWS,
            )
        )
        if turn == 0:
            for copy in matrix_copies:
                copy.wait()
            unpack(matrix_in, matrix_fields, MATRIX_GROUPS, MATRIX_ROWS)
            factor_chain()
        for copy in trips[0]:
            copy.wait()
        unpack(vector_in.at[trip], vector_fields, VECTOR_GROUPS, VECTOR_ROWS)
        solve_chain()
        trip = trip + 1
        pack(vector_fields, vector_out.at[trip], VECTOR_GROUPS, VECTOR_ROWS)
        answers = exchange(
            vector_out.at[trip],
            vector_in.at[trip],
            vector_send.at[trip],
            vector_recv.at[trip],
            VECTOR_ROWS,
        )
        for copy in answers:
            copy.wait()
        unpack(vector_in.at[trip], vector_fields, VECTOR_GROUPS, VECTOR_ROWS)
        below = get_vector(vector_fields, 0)
        own = get_vector(vector_fields, N)
        target = out if turn == SWEEPS - 1 else state
        for m in range(INNER):
            target[:, m] = partial[m] + matvec(spike_low[m], below) + matvec(spike_high[m], own)
        target[:, INNER] = own
        if turn < SWEEPS - 1:
            pending = exchange_halo(turn + 1)


def body(state_in, source, face_flux, time_term, inplane_coef):
    f32 = jnp.float32
    cell = (2, 128)
    anywhere = pl.BlockSpec(memory_space=pl.ANY)
    return pl.pallas_call(
        kernel,
        out_shape=jax.ShapeDtypeStruct(state_in.shape, f32),
        in_specs=[anywhere] * 5,
        out_specs=pl.BlockSpec(memory_space=pltpu.VMEM),
        scratch_shapes=[
            pltpu.VMEM((N, CELLS) + cell, f32),
            pltpu.VMEM((N, CELLS) + cell, f32),
            pltpu.VMEM((N, N, CELLS) + cell, f32),
            pltpu.VMEM((N, CELLS) + cell, f32),
            pltpu.VMEM((2, CELLS) + cell, f32),
            pltpu.VMEM((INNER, N, N) + cell, f32),
            pltpu.VMEM((INNER, N, N) + cell, f32),
            pltpu.VMEM((INNER, N, N) + cell, f32),
            pltpu.VMEM((INNER, N, N) + cell, f32),
            pltpu.VMEM((INNER, N, N) + cell, f32),
            pltpu.VMEM((INNER, N) + cell, f32),
            pltpu.VMEM((N, N) + cell, f32),
            pltpu.VMEM((4, N, N) + cell, f32),
            pltpu.VMEM((4, N, N) + cell, f32),
            pltpu.VMEM((4, N, N) + cell, f32),
            pltpu.VMEM((16 * MATRIX_GROUPS, 128), f32),
            pltpu.VMEM((16 * VECTOR_GROUPS, 128), f32),
            pltpu.VMEM((SEGS * MATRIX_ROWS, 128), f32),
            pltpu.VMEM((SEGS * MATRIX_ROWS, 128), f32),
            pltpu.VMEM((2 * SWEEPS, SEGS * VECTOR_ROWS, 128), f32),
            pltpu.VMEM((2 * SWEEPS, SEGS * VECTOR_ROWS, 128), f32),
            pltpu.VMEM((SWEEPS, 2, N, CELLS) + cell, f32),
            pltpu.SemaphoreType.DMA((5,)),
            pltpu.SemaphoreType.DMA((SEGS,)),
            pltpu.SemaphoreType.DMA((SEGS,)),
            pltpu.SemaphoreType.DMA((2 * SWEEPS, SEGS)),
            pltpu.SemaphoreType.DMA((2 * SWEEPS, SEGS)),
            pltpu.SemaphoreType.DMA((SWEEPS, 2)),
            pltpu.SemaphoreType.DMA((SWEEPS, 2)),
        ],
        compiler_params=pltpu.CompilerParams(collective_id=0, has_side_effects=True),
        name="line_relaxation",
    )(state_in, source, face_flux, time_term, inplane_coef)


def solution(mesh):
    return jax.shard_map(
        body,
        mesh=mesh,
        in_specs=(
            P(None, "wall", "band", None),
            P(None, "wall", "band", None),
            P(None, None, "wall", "band", None),
            P(None, "wall", "band", None),
            P(None, "wall", "band", None),
        ),
        out_specs=P(None, "wall", "band", None),
        check_vma=False,
    )
```

```python
import jax
import jax.numpy as jnp
from jax import lax
from jax.experimental import pallas as pl
from jax.experimental.pallas import tpu as pltpu
from jax.sharding import PartitionSpec as P

SWEEPS = 2
N = 5
CELLS = 8
INNER = CELLS - 1
SEGS = 16
MATRIX_GROUPS = 13
VECTOR_GROUPS = 2
MATRIX_ROWS = 16
MESH = pl.DeviceIdType.MESH


def matmul(left, right):
    total = left[:, 0:1] * right[0:1]
    for k in range(1, N):
        total = total + left[:, k : k + 1] * right[k : k + 1]
    return total


def matvec(matrix, vector):
    total = matrix[:, 0] * vector[0:1]
    for k in range(1, N):
        total = total + matrix[:, k] * vector[k : k + 1]
    return total


def with_entry(row, at, value):
    parts = []
    if at > 0:
        parts.append(row[:at])
    parts.append(value)
    if at < N - 1:
        parts.append(row[at + 1 :])
    return jnp.concatenate(parts, axis=0)


def invert(matrix):
    rows = [matrix[i] for i in range(N)]
    zero = jnp.zeros_like(rows[0][0:1])
    for p in range(N):
        scale = 1.0 / rows[p][p : p + 1]
        pivot_row = with_entry(rows[p] * scale, p, scale)
        updated = []
        for i in range(N):
            if i == p:
                updated.append(pivot_row)
            else:
                column = rows[i][p : p + 1]
                updated.append(with_entry(rows[i], p, zero) - column * pivot_row)
        rows = updated
    return jnp.stack(rows, axis=0)


def add_diagonal(matrix, diagonal):
    rows = [
        with_entry(matrix[i], i, matrix[i][i : i + 1] + diagonal[i : i + 1]) for i in range(N)
    ]
    return jnp.stack(rows, axis=0)


def one_minus(matrix):
    rows = [with_entry(-matrix[i], i, 1.0 - matrix[i][i : i + 1]) for i in range(N)]
    return jnp.stack(rows, axis=0)


def swap_rows(values):
    return jnp.concatenate([values[..., 1:2, :], values[..., 0:1, :]], axis=-2)


def lane_roll(values, shift):
    return pltpu.roll(values, shift % 128, values.ndim - 1)


def lane_of(values):
    return lax.broadcasted_iota(jnp.int32, values.shape, values.ndim - 1)


def row_of(values):
    return lax.broadcasted_iota(jnp.int32, values.shape, values.ndim - 2)


def segment_before(values, distance):
    if distance == 8:
        return swap_rows(values)
    rolled = lane_roll(values, 16 * distance)
    return jnp.where(lane_of(values) < 16 * distance, swap_rows(rolled), rolled)


def segment_after(values, distance):
    if distance == 8:
        return swap_rows(values)
    rolled = lane_roll(values, -16 * distance)
    return jnp.where(lane_of(values) >= 128 - 16 * distance, swap_rows(rolled), rolled)


def first_segment(values):
    return (row_of(values) == 0) & (lane_of(values) < 16)


def last_segment(values):
    return (row_of(values) == 1) & (lane_of(values) >= 112)


def transpose_groups(tile):
    sublane = row_of(tile)
    group = lane_of(tile) // 16
    for bit in (1, 2, 4):
        in_row = (sublane // bit) % 2 == 1
        in_lane = (group // bit) % 2 == 1
        from_next = lane_roll(pltpu.roll(tile, 8 - bit, 0), 16 * bit)
        if bit == 4:
            other = from_next
        else:
            from_prev = lane_roll(pltpu.roll(tile, bit, 0), -16 * bit)
            other = jnp.where(in_lane, from_next, from_prev)
        tile = jnp.where(in_row == in_lane, tile, other)
    return tile


def pack_matrices(fields, messages):
    for g in range(MATRIX_GROUPS):
        for r in range(2):
            tile = fields[pl.ds(16 * g + r, 8, stride=2), :]
            rows = pl.ds(8 * r * MATRIX_ROWS + g, 8, stride=MATRIX_ROWS)
            messages[rows, :] = transpose_groups(tile)


def unpack_matrices(messages, fields):
    for g in range(MATRIX_GROUPS):
        for r in range(2):
            tile = messages[pl.ds(8 * r * MATRIX_ROWS + g, 8, stride=MATRIX_ROWS), :]
            fields[pl.ds(16 * g + r, 8, stride=2), :] = transpose_groups(tile)


def pack_vectors(fields, messages):
    for r in range(2):
        for g in range(VECTOR_GROUPS):
            tile = fields[pl.ds(16 * g + r, 8, stride=2), :]
            messages[8 * r : 8 * r + 8, g, :] = transpose_groups(tile)


def unpack_vectors(messages, fields):
    for r in range(2):
        for g in range(VECTOR_GROUPS):
            tile = messages[8 * r : 8 * r + 8, g, :]
            fields[pl.ds(16 * g + r, 8, stride=2), :] = transpose_groups(tile)


def put_vector(fields, first, vector):
    for i in range(N):
        at = 2 * (first + i)
        fields[at : at + 2, :] = vector[i]


def get_vector(fields, first):
    return jnp.stack([fields[2 * (first + i) : 2 * (first + i) + 2, :] for i in range(N)], axis=0)


def put_matrix(fields, first, matrix):
    for i in range(N):
        put_vector(fields, first + N * i, matrix[i])


def get_matrix(fields, first):
    return jnp.stack([get_vector(fields, first + N * i) for i in range(N)], axis=0)


def kernel(
    state_in,
    source_in,
    face_in,
    time_in,
    coef_in,
    out,
    state,
    source,
    face,
    time,
    coef,
    held_inverse,
    held_lower,
    held_upper,
    spike_low,
    spike_high,
    partial,
    chain_inverse,
    round_inverse,
    round_lower,
    round_upper,
    matrix_fields,
    vector_fields,
    matrix_out,
    matrix_in,
    vector_out,
    vector_in,
    halo_in,
    load_sem,
    matrix_send,
    matrix_recv,
    vector_send,
    vector_recv,
    halo_send,
    halo_recv,
):
    wall = lax.axis_index("wall")
    band = lax.axis_index("band")
    bands = lax.axis_size("band")
    has_prev = band > 0
    has_next = band < bands - 1
    neighbours = ((has_next, band + 1), (has_prev, band - 1))

    barrier = pltpu.get_barrier_semaphore()
    for present, neighbour in neighbours:

        @pl.when(present)
        def _():
            pl.semaphore_signal(barrier, inc=1, device_id={"band": neighbour}, device_id_type=MESH)

    for offset in range(1, SEGS):
        pl.semaphore_signal(
            barrier,
            inc=1,
            device_id={"wall": lax.rem(wall + offset, SEGS)},
            device_id_type=MESH,
        )

    loads = [
        pltpu.make_async_copy(face_in, face, load_sem.at[0]),
        pltpu.make_async_copy(time_in, time, load_sem.at[1]),
        pltpu.make_async_copy(coef_in, coef, load_sem.at[2]),
        pltpu.make_async_copy(state_in, state, load_sem.at[3]),
        pltpu.make_async_copy(source_in, source, load_sem.at[4]),
    ]
    for load in loads:
        load.start()

    def exchange(send_from, land_in, send_sems, recv_sems, at):
        copies = []
        for offset in range(1, SEGS):
            there = lax.rem(wall + offset, SEGS)
            copy = pltpu.make_async_remote_copy(
                src_ref=send_from.at[at(there)],
                dst_ref=land_in.at[at(wall)],
                send_sem=send_sems.at[offset],
                recv_sem=recv_sems.at[offset],
                device_id={"wall": there},
                device_id_type=MESH,
            )
            copy.start()
            copies.append(copy)
        land_in[at(wall)] = send_from[at(wall)]
        return copies

    def matrix_at(segment):
        return pl.ds(pl.multiple_of(segment * MATRIX_ROWS, MATRIX_ROWS), MATRIX_ROWS)

    def vector_at(segment):
        return segment

    def halo_copy(turn, side):
        return pltpu.make_async_remote_copy(
            src_ref=state,
            dst_ref=halo_in.at[turn, side],
            send_sem=halo_send.at[turn, side],
            recv_sem=halo_recv.at[turn, side],
            device_id={"band": neighbours[side][1]},
            device_id_type=MESH,
        )

    def send_halo(turn):
        for side in range(2):

            @pl.when(neighbours[side][0])
            def _():
                halo_copy(turn, side).start()

    def wait_halo(turn):
        for side in range(2):

            @pl.when(neighbours[side][0])
            def _():
                halo_copy(turn, side).wait_send()
                halo_copy(turn, 1 - side).wait_recv()

    for load in loads[:3]:
        load.wait()

    upper = None
    spike = None
    for m in range(INNER):
        own_face = face[:, :, m]
        next_face = face[:, :, m + 1]
        center = time[:, m] + 2.5 * (coef[0:1, m] + coef[1:2, m])
        if m == 0:
            pivot = own_face + next_face
        else:
            pivot = next_face + matmul(own_face, one_minus(upper))
        inverse = invert(add_diagonal(pivot, center))
        lower = matmul(inverse, own_face)
        upper = matmul(inverse, next_face)
        spike = lower if m == 0 else matmul(lower, spike)
        held_inverse[m] = inverse
        held_lower[m] = lower
        held_upper[m] = upper
        spike_low[m] = spike
    spike_high[INNER - 1] = upper
    high = upper
    for m in range(INNER - 2, -1, -1):
        upper = held_upper[m]
        spike = spike_low[m] + matmul(upper, spike)
        high = matmul(upper, high)
        spike_low[m] = spike
        spike_high[m] = high

    first_face = face[:, :, 0]
    last_face = face[:, :, INNER]
    center = time[:, INNER] + 2.5 * (coef[0:1, INNER] + coef[1:2, INNER])
    put_matrix(matrix_fields, 0, matmul(first_face, one_minus(spike)))
    put_matrix(matrix_fields, 25, -matmul(first_face, high))
    put_matrix(matrix_fields, 50, -matmul(last_face, spike_low[INNER - 1]))
    put_matrix(
        matrix_fields,
        75,
        add_diagonal(matmul(last_face, one_minus(spike_high[INNER - 1])), center),
    )

    for load in loads[3:]:
        load.wait()
    pl.semaphore_wait(
        barrier, SEGS - 1 + has_prev.astype(jnp.int32) + has_next.astype(jnp.int32)
    )
    send_halo(0)
    pack_matrices(matrix_fields, matrix_out)
    matrix_copies = exchange(matrix_out, matrix_in, matrix_send, matrix_recv, matrix_at)

    def eliminate(turn):
        value = None
        for m in range(CELLS):
            here = state[:, m]
            before = jnp.where(has_prev, halo_in[turn, 0, :, m], 0.0)
            after = jnp.where(has_next, halo_in[turn, 1, :, m], 0.0)
            top = row_of(here) == 0
            along_i = (1.0 / 12.0) * (before + after) - (4.0 / 3.0) * swap_rows(
                here + jnp.where(top, after, before)
            )
            lane = lane_of(here)
            far = jnp.where(lane < 126, lane_roll(here, -2), 0.0) + jnp.where(
                lane >= 2, lane_roll(here, 2), 0.0
            )
            near = jnp.where(lane < 127, lane_roll(here, -1), 0.0) + jnp.where(
                lane >= 1, lane_roll(here, 1), 0.0
            )
            along_j = (1.0 / 12.0) * far - (4.0 / 3.0) * near
            target = source[:, m] - (coef[0:1, m] * along_i + coef[1:2, m] * along_j)
            if m == INNER:
                put_vector(vector_fields, N, target + matvec(face[:, :, INNER], value))
            else:
                fresh = matvec(held_inverse[m], target)
                value = fresh if m == 0 else fresh + matvec(held_lower[m], value)
                partial[m] = value
        for m in range(INNER - 2, -1, -1):
            value = partial[m] + matvec(held_upper[m], value)
            partial[m] = value
        put_vector(vector_fields, 0, matvec(face[:, :, 0], value))

    def factor_chain():
        from_above = []
        for first in (0, 25):
            block = segment_after(get_matrix(matrix_fields, first), 1)
            from_above.append(jnp.where(last_segment(block), 0.0, block))
        lower = get_matrix(matrix_fields, 50)
        lower = jnp.where(first_segment(lower), 0.0, lower)
        inverse = invert(get_matrix(matrix_fields, 75) + from_above[0])
        chain_inverse[...] = inverse
        lower = matmul(inverse, lower)
        upper = matmul(inverse, from_above[1])
        for step, distance in enumerate((1, 2, 4, 8)):
            upper_before = segment_before(upper, distance)
            lower_after = segment_after(lower, distance)
            inverse = invert(
                one_minus(matmul(lower, upper_before) + matmul(upper, lower_after))
            )
            low = matmul(inverse, lower)
            high = matmul(inverse, upper)
            round_inverse[step] = inverse
            round_lower[step] = low
            round_upper[step] = high
            if distance < 8:
                lower = -matmul(low, segment_before(lower, distance))
                upper = -matmul(high, segment_after(upper, distance))

    def solve_chain():
        from_above = segment_after(get_vector(vector_fields, 0), 1)
        from_above = jnp.where(last_segment(from_above), 0.0, from_above)
        value = matvec(chain_inverse[...], get_vector(vector_fields, N) + from_above)
        for step, distance in enumerate((1, 2, 4, 8)):
            value = (
                matvec(round_inverse[step], value)
                - matvec(round_lower[step], segment_before(value, distance))
                - matvec(round_upper[step], segment_after(value, distance))
            )
        before = segment_before(value, 1)
        put_vector(vector_fields, 0, jnp.where(first_segment(before), 0.0, before))
        put_vector(vector_fields, N, value)

    for turn in range(SWEEPS):
        wait_halo(turn)
        eliminate(turn)
        trips = []
        trip = 2 * turn
        pack_vectors(vector_fields, vector_out.at[trip])
        trips.append(
            exchange(
                vector_out.at[trip],
                vector_in.at[trip],
                vector_send.at[trip],
                vector_recv.at[trip],
                vector_at,
            )
        )
        if turn == 0:
            for copy in matrix_copies:
                copy.wait()
            unpack_matrices(matrix_in, matrix_fields)
            factor_chain()
        for copy in trips[0]:
            copy.wait()
        unpack_vectors(vector_in.at[trip], vector_fields)
        solve_chain()
        trip = trip + 1
        pack_vectors(vector_fields, vector_out.at[trip])
        answers = exchange(
            vector_out.at[trip],
            vector_in.at[trip],
            vector_send.at[trip],
            vector_recv.at[trip],
            vector_at,
        )
        for copy in answers:
            copy.wait()
        unpack_vectors(vector_in.at[trip], vector_fields)
        below = get_vector(vector_fields, 0)
        own = get_vector(vector_fields, N)
        target = out if turn == SWEEPS - 1 else state
        for m in range(INNER):
            target[:, m] = partial[m] + matvec(spike_low[m], below) + matvec(spike_high[m], own)
        target[:, INNER] = own
        if turn < SWEEPS - 1:
            send_halo(turn + 1)


def body(state_in, source, face_flux, time_term, inplane_coef):
    f32 = jnp.float32
    cell = (2, 128)
    anywhere = pl.BlockSpec(memory_space=pl.ANY)
    return pl.pallas_call(
        kernel,
        out_shape=pltpu.VMEM(state_in.shape, f32),
        in_specs=[anywhere] * 5,
        out_specs=pl.BlockSpec(memory_space=pltpu.VMEM),
        scratch_shapes=[
            pltpu.VMEM((N, CELLS) + cell, f32),
            pltpu.VMEM((N, CELLS) + cell, f32),
            pltpu.VMEM((N, N, CELLS) + cell, f32),
            pltpu.VMEM((N, CELLS) + cell, f32),
            pltpu.VMEM((2, CELLS) + cell, f32),
            pltpu.VMEM((INNER, N, N) + cell, f32),
            pltpu.VMEM((INNER, N, N) + cell, f32),
            pltpu.VMEM((INNER, N, N) + cell, f32),
            pltpu.VMEM((INNER, N, N) + cell, f32),
            pltpu.VMEM((INNER, N, N) + cell, f32),
            pltpu.VMEM((INNER, N) + cell, f32),
            pltpu.VMEM((N, N) + cell, f32),
            pltpu.VMEM((4, N, N) + cell, f32),
            pltpu.VMEM((4, N, N) + cell, f32),
            pltpu.VMEM((4, N, N) + cell, f32),
            pltpu.VMEM((16 * MATRIX_GROUPS, 128), f32),
            pltpu.VMEM((16 * VECTOR_GROUPS, 128), f32),
            pltpu.VMEM((SEGS * MATRIX_ROWS, 128), f32),
            pltpu.VMEM((SEGS * MATRIX_ROWS, 128), f32),
            pltpu.VMEM((2 * SWEEPS, SEGS, VECTOR_GROUPS, 128), f32),
            pltpu.VMEM((2 * SWEEPS, SEGS, VECTOR_GROUPS, 128), f32),
            pltpu.VMEM((SWEEPS, 2, N, CELLS) + cell, f32),
            pltpu.SemaphoreType.DMA((5,)),
            pltpu.SemaphoreType.DMA((SEGS,)),
            pltpu.SemaphoreType.DMA((SEGS,)),
            pltpu.SemaphoreType.DMA((2 * SWEEPS, SEGS)),
            pltpu.SemaphoreType.DMA((2 * SWEEPS, SEGS)),
            pltpu.SemaphoreType.DMA((SWEEPS, 2)),
            pltpu.SemaphoreType.DMA((SWEEPS, 2)),
        ],
        compiler_params=pltpu.CompilerParams(collective_id=0, has_side_effects=True),
        name="line_relaxation",
    )(state_in, source, face_flux, time_term, inplane_coef)


def solution(mesh):
    return jax.shard_map(
        body,
        mesh=mesh,
        in_specs=(
            P(None, "wall", "band", None),
            P(None, "wall", "band", None),
            P(None, None, "wall", "band", None),
            P(None, "wall", "band", None),
            P(None, "wall", "band", None),
        ),
        out_specs=P(None, "wall", "band", None),
        check_vma=False,
    )
```

```python
import jax
import jax.numpy as jnp
from jax import lax
from jax.experimental import pallas as pl
from jax.experimental.pallas import tpu as pltpu
from jax.sharding import PartitionSpec as P

SWEEPS = 2
N = 5
CELLS = 8
INNER = CELLS - 1
SEGS = 16
MATRIX_GROUPS = 13
VECTOR_GROUPS = 2
MATRIX_ROWS = 16
MESH = pl.DeviceIdType.MESH
FAR_FIRST = sorted(range(1, SEGS), key=lambda offset: -min(offset, SEGS - offset))


def matmul(left, right):
    total = left[:, 0:1] * right[0:1]
    for k in range(1, N):
        total = total + left[:, k : k + 1] * right[k : k + 1]
    return total


def matvec(matrix, vector):
    total = matrix[:, 0] * vector[0:1]
    for k in range(1, N):
        total = total + matrix[:, k] * vector[k : k + 1]
    return total


def with_entry(row, at, value):
    parts = []
    if at > 0:
        parts.append(row[:at])
    parts.append(value)
    if at < N - 1:
        parts.append(row[at + 1 :])
    return jnp.concatenate(parts, axis=0)


def invert(matrix):
    rows = [matrix[i] for i in range(N)]
    zero = jnp.zeros_like(rows[0][0:1])
    for p in range(N):
        scale = 1.0 / rows[p][p : p + 1]
        pivot_row = with_entry(rows[p] * scale, p, scale)
        updated = []
        for i in range(N):
            if i == p:
                updated.append(pivot_row)
            else:
                column = rows[i][p : p + 1]
                updated.append(with_entry(rows[i], p, zero) - column * pivot_row)
        rows = updated
    return jnp.stack(rows, axis=0)


def add_diagonal(matrix, diagonal):
    rows = [
        with_entry(matrix[i], i, matrix[i][i : i + 1] + diagonal[i : i + 1]) for i in range(N)
    ]
    return jnp.stack(rows, axis=0)


def one_minus(matrix):
    rows = [with_entry(-matrix[i], i, 1.0 - matrix[i][i : i + 1]) for i in range(N)]
    return jnp.stack(rows, axis=0)


def swap_rows(values):
    return jnp.concatenate([values[..., 1:2, :], values[..., 0:1, :]], axis=-2)


def lane_roll(values, shift):
    return pltpu.roll(values, shift % 128, values.ndim - 1)


def lane_of(values):
    return lax.broadcasted_iota(jnp.int32, values.shape, values.ndim - 1)


def row_of(values):
    return lax.broadcasted_iota(jnp.int32, values.shape, values.ndim - 2)


def segment_before(values, distance):
    if distance == 8:
        return swap_rows(values)
    rolled = lane_roll(values, 16 * distance)
    return jnp.where(lane_of(values) < 16 * distance, swap_rows(rolled), rolled)


def segment_after(values, distance):
    if distance == 8:
        return swap_rows(values)
    rolled = lane_roll(values, -16 * distance)
    return jnp.where(lane_of(values) >= 128 - 16 * distance, swap_rows(rolled), rolled)


def first_segment(values):
    return (row_of(values) == 0) & (lane_of(values) < 16)


def last_segment(values):
    return (row_of(values) == 1) & (lane_of(values) >= 112)


def transpose_groups(tile):
    sublane = row_of(tile)
    group = lane_of(tile) // 16
    for bit in (1, 2, 4):
        in_row = (sublane // bit) % 2 == 1
        in_lane = (group // bit) % 2 == 1
        from_next = lane_roll(pltpu.roll(tile, 8 - bit, 0), 16 * bit)
        if bit == 4:
            other = from_next
        else:
            from_prev = lane_roll(pltpu.roll(tile, bit, 0), -16 * bit)
            other = jnp.where(in_lane, from_next, from_prev)
        tile = jnp.where(in_row == in_lane, tile, other)
    return tile


def pack_matrices(fields, messages):
    for g in range(MATRIX_GROUPS):
        for r in range(2):
            tile = fields[pl.ds(16 * g + r, 8, stride=2), :]
            rows = pl.ds(8 * r * MATRIX_ROWS + g, 8, stride=MATRIX_ROWS)
            messages[rows, :] = transpose_groups(tile)


def unpack_matrices(messages, fields):
    for g in range(MATRIX_GROUPS):
        for r in range(2):
            tile = messages[pl.ds(8 * r * MATRIX_ROWS + g, 8, stride=MATRIX_ROWS), :]
            fields[pl.ds(16 * g + r, 8, stride=2), :] = transpose_groups(tile)


def pack_vectors(fields, messages):
    for r in range(2):
        for g in range(VECTOR_GROUPS):
            tile = fields[pl.ds(16 * g + r, 8, stride=2), :]
            messages[8 * r : 8 * r + 8, g, :] = transpose_groups(tile)


def unpack_vectors(messages, fields):
    for r in range(2):
        for g in range(VECTOR_GROUPS):
            tile = messages[8 * r : 8 * r + 8, g, :]
            fields[pl.ds(16 * g + r, 8, stride=2), :] = transpose_groups(tile)


def put_vector(fields, first, vector):
    for i in range(N):
        at = 2 * (first + i)
        fields[at : at + 2, :] = vector[i]


def get_vector(fields, first):
    return jnp.stack([fields[2 * (first + i) : 2 * (first + i) + 2, :] for i in range(N)], axis=0)


def put_matrix(fields, first, matrix):
    for i in range(N):
        put_vector(fields, first + N * i, matrix[i])


def get_matrix(fields, first):
    return jnp.stack([get_vector(fields, first + N * i) for i in range(N)], axis=0)


def kernel(
    state_in,
    source_in,
    face_in,
    time_in,
    coef_in,
    out,
    state,
    source,
    face,
    time,
    coef,
    held_inverse,
    held_lower,
    held_upper,
    spikes,
    partial,
    chain_inverse,
    round_inverse,
    round_lower,
    round_upper,
    matrix_fields,
    vector_fields,
    matrix_out,
    matrix_in,
    vector_out,
    vector_in,
    halo_in,
    near_spikes,
    near_partial,
    near_answers,
    near_fields,
    load_sem,
    matrix_send,
    matrix_recv,
    vector_send,
    vector_recv,
    halo_send,
    halo_recv,
    near_send,
    near_recv,
    answer_send,
    answer_recv,
):
    spike_low = spikes.at[0]
    spike_high = spikes.at[1]
    wall = lax.axis_index("wall")
    band = lax.axis_index("band")
    bands = lax.axis_size("band")
    has_prev = band > 0
    has_next = band < bands - 1
    neighbours = ((has_next, band + 1), (has_prev, band - 1))

    barrier = pltpu.get_barrier_semaphore()
    for present, neighbour in neighbours:

        @pl.when(present)
        def _():
            pl.semaphore_signal(barrier, inc=1, device_id={"band": neighbour}, device_id_type=MESH)

    for offset in range(1, SEGS):
        pl.semaphore_signal(
            barrier,
            inc=1,
            device_id={"wall": lax.rem(wall + offset, SEGS)},
            device_id_type=MESH,
        )

    loads = [
        pltpu.make_async_copy(face_in, face, load_sem.at[0]),
        pltpu.make_async_copy(time_in, time, load_sem.at[1]),
        pltpu.make_async_copy(coef_in, coef, load_sem.at[2]),
        pltpu.make_async_copy(state_in, state, load_sem.at[3]),
        pltpu.make_async_copy(source_in, source, load_sem.at[4]),
    ]
    for load in loads:
        load.start()

    def exchange(send_from, land_in, send_sems, recv_sems, at):
        copies = []
        for offset in FAR_FIRST:
            there = lax.rem(wall + offset, SEGS)
            copy = pltpu.make_async_remote_copy(
                src_ref=send_from.at[at(there)],
                dst_ref=land_in.at[at(wall)],
                send_sem=send_sems.at[offset],
                recv_sem=recv_sems.at[offset],
                device_id={"wall": there},
                device_id_type=MESH,
            )
            copy.start()
            copies.append(copy)
        land_in[at(wall)] = send_from[at(wall)]
        return copies[::-1]

    def matrix_at(segment):
        return pl.ds(pl.multiple_of(segment * MATRIX_ROWS, MATRIX_ROWS), MATRIX_ROWS)

    def vector_at(segment):
        return segment

    def halo_copy(turn, side):
        return pltpu.make_async_remote_copy(
            src_ref=state,
            dst_ref=halo_in.at[turn, side],
            send_sem=halo_send.at[turn, side],
            recv_sem=halo_recv.at[turn, side],
            device_id={"band": neighbours[side][1]},
            device_id_type=MESH,
        )

    def send_halo(turn):
        for side in range(2):

            @pl.when(neighbours[side][0])
            def _():
                halo_copy(turn, side).start()

    def wait_halo(turn):
        for side in range(2):

            @pl.when(neighbours[side][0])
            def _():
                halo_copy(turn, side).wait_send()
                halo_copy(turn, 1 - side).wait_recv()

    def near_copy(kind, side):
        source_ref, landing = ((spikes, near_spikes), (partial, near_partial))[kind]
        return pltpu.make_async_remote_copy(
            src_ref=source_ref,
            dst_ref=landing.at[side],
            send_sem=near_send.at[kind, side],
            recv_sem=near_recv.at[kind, side],
            device_id={"band": neighbours[side][1]},
            device_id_type=MESH,
        )

    def send_near(kind):
        for side in range(2):

            @pl.when(neighbours[side][0])
            def _():
                near_copy(kind, side).start()

    def answer_copy(answers, side, offset):
        there = lax.rem(wall + offset, SEGS)
        return pltpu.make_async_remote_copy(
            src_ref=answers.at[there],
            dst_ref=near_answers.at[side, wall],
            send_sem=answer_send.at[side, offset],
            recv_sem=answer_recv.at[side, offset],
            device_id={"band": neighbours[side][1], "wall": there},
            device_id_type=MESH,
        )

    def send_answers(answers):
        for side in range(2):

            @pl.when(neighbours[side][0])
            def _():
                for offset in FAR_FIRST + [0]:
                    answer_copy(answers, side, offset).start()

    def wait_near(answers):
        for side in range(2):

            @pl.when(neighbours[side][0])
            def _():
                for kind in range(2):
                    near_copy(kind, side).wait_send()
                    near_copy(kind, 1 - side).wait_recv()
                for offset in [0] + FAR_FIRST[::-1]:
                    answer_copy(answers, side, offset).wait_send()
                    answer_copy(answers, 1 - side, offset).wait_recv()

    for load in loads[:3]:
        load.wait()

    upper = None
    spike = None
    for m in range(INNER):
        own_face = face[:, :, m]
        next_face = face[:, :, m + 1]
        center = time[:, m] + 2.5 * (coef[0:1, m] + coef[1:2, m])
        if m == 0:
            pivot = own_face + next_face
        else:
            pivot = next_face + matmul(own_face, one_minus(upper))
        inverse = invert(add_diagonal(pivot, center))
        lower = matmul(inverse, own_face)
        upper = matmul(inverse, next_face)
        spike = lower if m == 0 else matmul(lower, spike)
        held_inverse[m] = inverse
        held_lower[m] = lower
        held_upper[m] = upper
        spike_low[m] = spike
    spike_high[INNER - 1] = upper
    high = upper
    for m in range(INNER - 2, -1, -1):
        upper = held_upper[m]
        spike = spike_low[m] + matmul(upper, spike)
        high = matmul(upper, high)
        spike_low[m] = spike
        spike_high[m] = high

    first_face = face[:, :, 0]
    last_face = face[:, :, INNER]
    center = time[:, INNER] + 2.5 * (coef[0:1, INNER] + coef[1:2, INNER])
    put_matrix(matrix_fields, 0, matmul(first_face, one_minus(spike)))
    put_matrix(matrix_fields, 25, -matmul(first_face, high))
    put_matrix(matrix_fields, 50, -matmul(last_face, spike_low[INNER - 1]))
    put_matrix(
        matrix_fields,
        75,
        add_diagonal(matmul(last_face, one_minus(spike_high[INNER - 1])), center),
    )

    for load in loads[3:]:
        load.wait()
    pl.semaphore_wait(
        barrier, SEGS - 1 + has_prev.astype(jnp.int32) + has_next.astype(jnp.int32)
    )
    send_halo(0)
    pack_matrices(matrix_fields, matrix_out)
    matrix_copies = exchange(matrix_out, matrix_in, matrix_send, matrix_recv, matrix_at)
    send_near(0)

    def eliminate(turn):
        value = None
        for m in range(CELLS):
            here = state[:, m]
            before = jnp.where(has_prev, halo_in[turn, 0, :, m], 0.0)
            after = jnp.where(has_next, halo_in[turn, 1, :, m], 0.0)
            top = row_of(here) == 0
            along_i = (1.0 / 12.0) * (before + after) - (4.0 / 3.0) * swap_rows(
                here + jnp.where(top, after, before)
            )
            lane = lane_of(here)
            far = jnp.where(lane < 126, lane_roll(here, -2), 0.0) + jnp.where(
                lane >= 2, lane_roll(here, 2), 0.0
            )
            near = jnp.where(lane < 127, lane_roll(here, -1), 0.0) + jnp.where(
                lane >= 1, lane_roll(here, 1), 0.0
            )
            along_j = (1.0 / 12.0) * far - (4.0 / 3.0) * near
            target = source[:, m] - (coef[0:1, m] * along_i + coef[1:2, m] * along_j)
            if m == INNER:
                put_vector(vector_fields, N, target + matvec(face[:, :, INNER], value))
            else:
                fresh = matvec(held_inverse[m], target)
                value = fresh if m == 0 else fresh + matvec(held_lower[m], value)
                partial[m] = value
        for m in range(INNER - 2, -1, -1):
            value = partial[m] + matvec(held_upper[m], value)
            partial[m] = value
        put_vector(vector_fields, 0, matvec(face[:, :, 0], value))

    def factor_chain():
        from_above = []
        for first in (0, 25):
            block = segment_after(get_matrix(matrix_fields, first), 1)
            from_above.append(jnp.where(last_segment(block), 0.0, block))
        lower = get_matrix(matrix_fields, 50)
        lower = jnp.where(first_segment(lower), 0.0, lower)
        inverse = invert(get_matrix(matrix_fields, 75) + from_above[0])
        chain_inverse[...] = inverse
        lower = matmul(inverse, lower)
        upper = matmul(inverse, from_above[1])
        for step, distance in enumerate((1, 2, 4, 8)):
            upper_before = segment_before(upper, distance)
            lower_after = segment_after(lower, distance)
            inverse = invert(
                one_minus(matmul(lower, upper_before) + matmul(upper, lower_after))
            )
            low = matmul(inverse, lower)
            high = matmul(inverse, upper)
            round_inverse[step] = inverse
            round_lower[step] = low
            round_upper[step] = high
            if distance < 8:
                lower = -matmul(low, segment_before(lower, distance))
                upper = -matmul(high, segment_after(upper, distance))

    def solve_chain():
        from_above = segment_after(get_vector(vector_fields, 0), 1)
        from_above = jnp.where(last_segment(from_above), 0.0, from_above)
        value = matvec(chain_inverse[...], get_vector(vector_fields, N) + from_above)
        for step, distance in enumerate((1, 2, 4, 8)):
            value = (
                matvec(round_inverse[step], value)
                - matvec(round_lower[step], segment_before(value, distance))
                - matvec(round_upper[step], segment_after(value, distance))
            )
        before = segment_before(value, 1)
        put_vector(vector_fields, 0, jnp.where(first_segment(before), 0.0, before))
        put_vector(vector_fields, N, value)

    def answer(target, fields, value, low_spike, high_spike):
        below = get_vector(fields, 0)
        own = get_vector(fields, N)
        for m in range(INNER):
            target[:, m] = value[m] + matvec(low_spike[m], below) + matvec(high_spike[m], own)
        target[:, INNER] = own

    wait_halo(0)
    for turn in range(SWEEPS):
        eliminate(turn)
        trip = 2 * turn
        pack_vectors(vector_fields, vector_out.at[trip])
        demands = exchange(
            vector_out.at[trip],
            vector_in.at[trip],
            vector_send.at[trip],
            vector_recv.at[trip],
            vector_at,
        )
        if turn == 0:
            send_near(1)
            for copy in matrix_copies:
                copy.wait()
            unpack_matrices(matrix_in, matrix_fields)
            factor_chain()
        for copy in demands:
            copy.wait()
        unpack_vectors(vector_in.at[trip], vector_fields)
        solve_chain()
        trip = trip + 1
        pack_vectors(vector_fields, vector_out.at[trip])
        if turn == 0:
            send_answers(vector_out.at[trip])
        answers = exchange(
            vector_out.at[trip],
            vector_in.at[trip],
            vector_send.at[trip],
            vector_recv.at[trip],
            vector_at,
        )
        for copy in answers:
            copy.wait()
        unpack_vectors(vector_in.at[trip], vector_fields)
        answer(out if turn == SWEEPS - 1 else state, vector_fields, partial, spike_low, spike_high)
        if turn == 0:
            wait_near(vector_out.at[trip])
            for side in range(2):
                fields = near_fields.at[side]
                unpack_vectors(near_answers.at[side], fields)
                answer(
                    halo_in.at[1, side],
                    fields,
                    near_partial.at[side],
                    near_spikes.at[side, 0],
                    near_spikes.at[side, 1],
                )


def body(state_in, source, face_flux, time_term, inplane_coef):
    f32 = jnp.float32
    cell = (2, 128)
    anywhere = pl.BlockSpec(memory_space=pl.ANY)
    return pl.pallas_call(
        kernel,
        out_shape=pltpu.VMEM(state_in.shape, f32),
        in_specs=[anywhere] * 5,
        out_specs=pl.BlockSpec(memory_space=pltpu.VMEM),
        scratch_shapes=[
            pltpu.VMEM((N, CELLS) + cell, f32),
            pltpu.VMEM((N, CELLS) + cell, f32),
            pltpu.VMEM((N, N, CELLS) + cell, f32),
            pltpu.VMEM((N, CELLS) + cell, f32),
            pltpu.VMEM((2, CELLS) + cell, f32),
            pltpu.VMEM((INNER, N, N) + cell, f32),
            pltpu.VMEM((INNER, N, N) + cell, f32),
            pltpu.VMEM((INNER, N, N) + cell, f32),
            pltpu.VMEM((2, INNER, N, N) + cell, f32),
            pltpu.VMEM((INNER, N) + cell, f32),
            pltpu.VMEM((N, N) + cell, f32),
            pltpu.VMEM((4, N, N) + cell, f32),
            pltpu.VMEM((4, N, N) + cell, f32),
            pltpu.VMEM((4, N, N) + cell, f32),
            pltpu.VMEM((16 * MATRIX_GROUPS, 128), f32),
            pltpu.VMEM((16 * VECTOR_GROUPS, 128), f32),
            pltpu.VMEM((SEGS * MATRIX_ROWS, 128), f32),
            pltpu.VMEM((SEGS * MATRIX_ROWS, 128), f32),
            pltpu.VMEM((2 * SWEEPS, SEGS, VECTOR_GROUPS, 128), f32),
            pltpu.VMEM((2 * SWEEPS, SEGS, VECTOR_GROUPS, 128), f32),
            pltpu.VMEM((SWEEPS, 2, N, CELLS) + cell, f32),
            pltpu.VMEM((2, 2, INNER, N, N) + cell, f32),
            pltpu.VMEM((2, INNER, N) + cell, f32),
            pltpu.VMEM((2, SEGS, VECTOR_GROUPS, 128), f32),
            pltpu.VMEM((2, 16 * VECTOR_GROUPS, 128), f32),
            pltpu.SemaphoreType.DMA((5,)),
            pltpu.SemaphoreType.DMA((SEGS,)),
            pltpu.SemaphoreType.DMA((SEGS,)),
            pltpu.SemaphoreType.DMA((2 * SWEEPS, SEGS)),
            pltpu.SemaphoreType.DMA((2 * SWEEPS, SEGS)),
            pltpu.SemaphoreType.DMA((SWEEPS, 2)),
            pltpu.SemaphoreType.DMA((SWEEPS, 2)),
            pltpu.SemaphoreType.DMA((2, 2)),
            pltpu.SemaphoreType.DMA((2, 2)),
            pltpu.SemaphoreType.DMA((2, SEGS)),
            pltpu.SemaphoreType.DMA((2, SEGS)),
        ],
        compiler_params=pltpu.CompilerParams(collective_id=0, has_side_effects=True),
        name="line_relaxation",
    )(state_in, source, face_flux, time_term, inplane_coef)


def solution(mesh):
    return jax.shard_map(
        body,
        mesh=mesh,
        in_specs=(
            P(None, "wall", "band", None),
            P(None, "wall", "band", None),
            P(None, None, "wall", "band", None),
            P(None, "wall", "band", None),
            P(None, "wall", "band", None),
        ),
        out_specs=P(None, "wall", "band", None),
        check_vma=False,
    )
```
